128 devices in a mesh: grid: 32 (over y, z, core), elem: 4 (over x).
Axes of the slice: x: 4, y: 4, z: 4, core: 2. Of those that a mesh axis runs over, the one named last changes fastest.
Arguments:
- jacobians: bfloat16 [4096, 320, 320], P(('grid', 'elem'))
- residual: bfloat16 [4096, 320], P(('grid', 'elem')), may hold values from -6 to 6
- owner_map: int32 [4096], P(('grid', 'elem')), may hold values from -1 to 31, as said below
- owner_slot: int32 [2048], P(('grid', 'elem')), may hold values from 0 to 31, as said below
- face_coupling: bfloat16 [320, 1920], replicated, may hold values from -0.109375 to 0.109375
- neighbours: int32 [6, 4096], P(None, ('grid', 'elem')), may hold values from -1 to 127, as said below
- donors: int32 [8192], P(('grid', 'elem')), may hold values from -1 to 31, as said below
- receptors: int32 [3, 16384], P(None, ('grid', 'elem')), may hold values from 0 to 63, as said below
- receptor_coords: float32 [3, 16384], P(None, ('grid', 'elem')), may hold values from -1 to 1
Outputs:
- precond: bfloat16 [2048, 320, 320], P(('grid', 'elem'))
- update: float32 [4096, 320], P(('grid', 'elem'))
The draws below stay inside these ranges and needn't reach their ends.
Inputs may be any that keep to these rules, and one draw needn't show every extreme that they name: `owner_map`: entry -1 marks an empty slot; a live entry g' + k sends the element to the device of grid index g' with the same elem index, as the k-th of at most 1 elements from this device to that one; a device uses each entry value at most once. A quarter of the grids, drawn from the seed, fill all 32 slots of their devices and send exactly 1 elements to every owner; the other grids' devices hold about a third as many. `owner_slot`: each device lists 16 distinct grid indices g, exactly those from whose device with the same elem index a live element arrives. `neighbours`: entry [f, n] of a live element names its neighbour across face f as e * 32 + s, slot s of the device with elem index e and the same grid index, or -1 at a boundary; the neighbour is live and names n back across face f xor 1. Empty slots hold -1. `donors`: on a device of grid index h, entry g * 2 + k names a live slot of that device, the k-th donor element for grid g; entries with g = h are -1. `receptors`: row 0 is a donor row h * 2 + k with h not the device's own grid index; row 1 a live slot of the device; row 2 a solution point index below 64.
All inputs are finite; a program needn't handle non-finite values.
Results may differ from the reference program's by a relative error of at most 0.0058.
Values may be sent and summed in bfloat16 or wider, within the bound.
A program may use at most 192 MiB of HBM per device.

```python
import jax
import jax.numpy as jnp
from jax import lax

VARS = 5
NODES = 4
PTS = 64
B = 320
OWN = 16
SLOTS = 32
CAP = 1
DCAP = 2
RPTS = 128
NS_ITERS = 3
N_GRID = 32
N_ELEM = 4
DEVICES = 128


def layout_maps(key):
    base = jax.random.fold_in(key, 11)
    key_order, key_shift, key_slots, key_recv = jax.random.split(base, 4)
    heavy_count = N_GRID // 4
    light_count = N_GRID - heavy_count
    units = OWN // 2
    grid_order = jax.random.permutation(key_order, N_GRID)
    grid_rank = jnp.argsort(grid_order)
    shifts = jax.random.randint(key_shift, (N_ELEM,), 0, light_count)
    light_row = (jnp.arange(N_GRID)[None, :, None] * units + jnp.arange(units)[None, None, :] + shifts[:, None, None]) % light_count
    light_load = jnp.sum((light_row[:, None, :, :] == jnp.arange(light_count)[None, :, None, None]).astype(jnp.int32), axis=3)
    light_pick = jnp.take(light_load, jnp.clip(grid_rank - heavy_count, 0, light_count - 1), axis=1)
    loads = jnp.where((grid_rank < heavy_count)[None, :, None], CAP, light_pick)
    send_load = loads.transpose(1, 0, 2).reshape(DEVICES, N_GRID)
    recv_load = loads.transpose(2, 0, 1).reshape(DEVICES, N_GRID)
    pair_rank = jnp.arange(CAP)
    send_live = (pair_rank[None, None, :] < send_load[:, :, None]).reshape(DEVICES, SLOTS)
    recv_live = (pair_rank[None, None, :] < recv_load[:, :, None]).reshape(DEVICES, SLOTS)
    slot_iota = jnp.arange(SLOTS)[None, :]
    live_first = jnp.argsort(jnp.where(send_live, slot_iota, SLOTS + slot_iota), axis=1)
    live_total = jnp.sum(send_live.astype(jnp.int32), axis=1)
    slot_keys = jax.random.randint(key_slots, (DEVICES, SLOTS), 0, 2 ** 16) * SLOTS + slot_iota
    slot_perm = jnp.argsort(slot_keys, axis=1)
    entry = jnp.where(slot_iota < live_total[:, None], live_first, -1)
    owner_map = jnp.zeros((DEVICES, SLOTS), jnp.int32).at[jnp.arange(DEVICES)[:, None], slot_perm].set(entry.astype(jnp.int32))
    recv_keys = jax.random.randint(key_recv, (DEVICES, SLOTS), 0, 2 ** 16) * SLOTS + slot_iota
    recv_order = jnp.argsort(jnp.where(recv_live, recv_keys, 2 ** 16 * SLOTS + recv_keys), axis=1)
    owner_slot = recv_order[:, :OWN]
    return (owner_map, owner_slot.astype(jnp.int32))


def live_lists(key):
    owner_map, unused_slot = layout_maps(key)
    live_slots = owner_map >= 0
    slot_iota = jnp.arange(SLOTS)[None, :]
    live_first = jnp.argsort(jnp.where(live_slots, slot_iota, SLOTS + slot_iota), axis=1)
    live_total = jnp.sum(live_slots.astype(jnp.int32), axis=1)
    return (live_first, live_total)


def draw_owner_map(key, part):
    owner_map, owner_slot = layout_maps(key)
    return owner_map.reshape(-1).astype(jnp.int32)


def draw_owner_slot(key, part):
    owner_map, owner_slot = layout_maps(key)
    return owner_slot.reshape(-1).astype(jnp.int32)


def draw_neighbours(key, part):
    owner_map, unused_slot = layout_maps(key)
    group_size = N_ELEM * SLOTS
    live_slots = (owner_map >= 0).reshape(N_GRID, group_size)
    group_iota = jnp.arange(group_size)[None, :]
    live_total = jnp.sum(live_slots.astype(jnp.int32), axis=1)[:, None]
    faces = []
    for direction in range(3):
        key_score, key_cut = jax.random.split(jax.random.fold_in(key, 21 + direction))
        scores = jax.random.randint(key_score, (N_GRID, group_size), 0, 2 ** 12) * group_size + group_iota
        scores = jnp.where(live_slots, scores, 2 ** 12 * group_size + group_iota)
        cycle_order = jnp.argsort(scores, axis=1)
        cycle_rank = jnp.argsort(cycle_order, axis=1)
        after = jnp.take_along_axis(cycle_order, (cycle_rank + 1) % live_total, axis=1)
        before = jnp.take_along_axis(cycle_order, (cycle_rank + live_total - 1) % live_total, axis=1)
        cut_mark = jax.random.randint(key_cut, (N_GRID, group_size), 0, 10) == 0
        cut_before = jnp.take_along_axis(cut_mark, before, axis=1)
        faces.append(jnp.where(live_slots & jnp.logical_not(cut_mark), after, -1))
        faces.append(jnp.where(live_slots & jnp.logical_not(cut_before), before, -1))
    return jnp.stack(faces).reshape(6, DEVICES * SLOTS).astype(jnp.int32)


def draw_donors(key, part):
    live_first, live_total = live_lists(key)
    pick = jax.random.randint(jax.random.fold_in(key, 31), (DEVICES, N_GRID * DCAP), 0, 2 ** 16) % live_total[:, None]
    chosen = jnp.take_along_axis(live_first, pick, axis=1)
    own_grid = jnp.arange(DEVICES) // N_ELEM
    target_grid = jnp.arange(N_GRID * DCAP) // DCAP
    return jnp.where(target_grid[None, :] == own_grid[:, None], -1, chosen).reshape(-1).astype(jnp.int32)


def draw_receptors(key, part):
    live_first, live_total = live_lists(key)
    key_shift, key_rank, key_point, key_slot = jax.random.split(jax.random.fold_in(key, 41), 4)
    own_grid = (jnp.arange(DEVICES) // N_ELEM)[:, None]
    shift = jax.random.randint(key_shift, (DEVICES, RPTS), 0, N_GRID - 1)
    rank = jax.random.randint(key_rank, (DEVICES, RPTS), 0, DCAP)
    point = jax.random.randint(key_point, (DEVICES, RPTS), 0, PTS)
    first = (jnp.arange(RPTS) == 0)[None, :]
    second = (jnp.arange(RPTS) == 1)[None, :]
    shift = jnp.where(first, N_GRID - 2, jnp.where(second, 0, shift))
    rank = jnp.where(first, DCAP - 1, jnp.where(second, 0, rank))
    point = jnp.where(first, PTS - 1, jnp.where(second, 0, point))
    source = (own_grid + 1 + shift) % N_GRID
    donor_row = source * DCAP + rank
    pick = jax.random.randint(key_slot, (DEVICES, RPTS), 0, 2 ** 16) % live_total[:, None]
    target_slot = jnp.take_along_axis(live_first, pick, axis=1)
    return jnp.stack([donor_row, target_slot, point]).reshape(3, DEVICES * RPTS).astype(jnp.int32)


def draw_jacobians(key, part):
    key_diag, key_off = jax.random.split(jax.random.fold_in(key, 51))
    count = DEVICES * SLOTS
    diagonal = jax.random.uniform(key_diag, (count, B), jnp.float32, 1.0, 2.0)
    coupling = jax.random.normal(key_off, (count, B, B), jnp.float32) * 0.05
    blocks = coupling + jnp.eye(B, dtype=jnp.float32)[None] * diagonal[:, None, :]
    return blocks.astype(jnp.bfloat16)


def shard_levels(own_key, dims, shards, low, top_value):
    factor_of = 1.0
    for dim, parts in shards:
        heights = jax.random.uniform(jax.random.fold_in(jax.random.fold_in(own_key, 6), dim), (parts,), jnp.float32, low / len(shards), top_value / len(shards))
        factor_of = factor_of * jnp.repeat(jnp.exp(heights), dims[dim] // parts).reshape((-1,) + (1,) * (len(dims) - 1 - dim))
    return factor_of


def scatter_about(rng, shape, width, bound, cuts=(), kind=jnp.bfloat16):
    factor_of = shard_levels(rng, shape, cuts, -0.22, 0.18) if cuts else 1.0
    array = jax.random.normal(rng, shape, jnp.float32) * width * factor_of
    return jnp.minimum(jnp.maximum(array, -bound), bound).astype(kind)


def setup_inputs(seed: int = 0) -> dict:
    seeds = jax.random.split(jax.random.key(seed), 10)
    jacobians = draw_jacobians(jax.random.fold_in(seeds[9], 71), 0)
    residual = scatter_about(seeds[1], (DEVICES * SLOTS, B), 1.0, 6.0, ((0, 128),))
    owner_map = draw_owner_map(jax.random.fold_in(seeds[9], 71), 0)
    owner_slot = draw_owner_slot(jax.random.fold_in(seeds[9], 71), 0)
    face_coupling = scatter_about(seeds[4], (B, 6 * B), (9 * B) ** -0.5, 0.109375)
    neighbours = draw_neighbours(jax.random.fold_in(seeds[9], 71), 0)
    donors = draw_donors(jax.random.fold_in(seeds[9], 71), 0)
    receptors = draw_receptors(jax.random.fold_in(seeds[9], 71), 0)
    receptor_coords = jnp.clip(jax.random.uniform(seeds[8], (3, DEVICES * RPTS), jnp.float32, -1.0, 1.0) * shard_levels(seeds[8], (3, DEVICES * RPTS), ((1, 128),), -0.4, 0.0), -1.0, 1.0)
    return {"jacobians": jacobians, "residual": residual, "owner_map": owner_map, "owner_slot": owner_slot, "face_coupling": face_coupling, "neighbours": neighbours, "donors": donors, "receptors": receptors, "receptor_coords": receptor_coords}


def basis_weights(receptor_coords):
    node_places = -jnp.cos(jnp.pi * jnp.arange(NODES, dtype=jnp.float32) / (NODES - 1))
    diagonal_mask = jnp.eye(NODES, dtype=bool)
    node_gaps = jnp.where(diagonal_mask, jnp.float32(1.0), node_places[:, None] - node_places[None, :])
    denominator = jnp.prod(node_gaps, axis=1)
    factors = []
    for direction in range(3):
        position = receptor_coords[direction]
        offsets = position[None, :] - node_places[:, None]
        numerator = jnp.prod(jnp.where(diagonal_mask[:, :, None], jnp.float32(1.0), offsets[None, :, :]), axis=1)
        factors.append(numerator / denominator[:, None])
    table = factors[0][:, None, None, :] * factors[1][None, :, None, :] * factors[2][None, None, :, :]
    return table.reshape(NODES ** 3, -1)


def invert_blocks(blocks):
    matrix = blocks.astype(jnp.float32)
    diagonal = jnp.diagonal(matrix, axis1=-2, axis2=-1)
    identity = jnp.eye(matrix.shape[-1], dtype=jnp.float32)
    approx = identity[None] / diagonal[:, None, :]
    for iteration in range(NS_ITERS):
        product = jnp.einsum("oij,ojk->oik", matrix, approx, precision=lax.Precision.HIGHEST)
        approx = 2.0 * approx - jnp.einsum("oij,ojk->oik", approx, product, precision=lax.Precision.HIGHEST)
    return approx.astype(jnp.bfloat16)


def apply_blocks(operands):
    block_set, vectors = operands
    return jnp.einsum("obc,oc->ob", block_set.astype(jnp.float32), vectors.astype(jnp.float32), precision=lax.Precision.HIGHEST)


def reference(jacobians, residual, owner_map, owner_slot, face_coupling, neighbours, donors, receptors, receptor_coords):
    total_slots = DEVICES * SLOTS
    device_of = jnp.arange(total_slots, dtype=jnp.int32) // SLOTS
    grid_of = device_of // N_ELEM
    elem_of = device_of % N_ELEM
    live_slots = owner_map >= 0
    routed = jnp.where(live_slots, owner_map, 0)
    arrival = ((routed // CAP) * N_ELEM + elem_of) * SLOTS + grid_of * CAP + routed % CAP
    arrival = jnp.where(live_slots, arrival, total_slots)
    arrival_table = jnp.zeros((total_slots + 1,), jnp.int32).at[arrival].set(jnp.arange(total_slots, dtype=jnp.int32))[:total_slots]
    holder = jnp.arange(DEVICES * OWN, dtype=jnp.int32) // OWN
    owned_native = arrival_table[holder * SLOTS + owner_slot]
    blocks_owned = jacobians[owned_native].reshape(DEVICES, OWN, B, B)
    precond = lax.map(invert_blocks, blocks_owned)
    rhs_owned = residual[owned_native].reshape(DEVICES, OWN, B)
    guess_owned = lax.map(apply_blocks, (precond, rhs_owned)).astype(jnp.bfloat16).reshape(DEVICES * OWN, B)
    own_of_native = jnp.zeros((total_slots,), jnp.int32).at[owned_native].set(jnp.arange(DEVICES * OWN, dtype=jnp.int32))
    first_guess = guess_owned[own_of_native]
    face_terms = jnp.dot(first_guess, face_coupling, preferred_element_type=jnp.float32).astype(jnp.bfloat16).reshape(total_slots, 6, B)
    group_base = grid_of * (N_ELEM * SLOTS)
    face_sum = jnp.zeros((total_slots, B), jnp.float32)
    for face_index in range(6):
        neighbour = neighbours[face_index]
        face_rows = face_terms[jnp.where(neighbour >= 0, group_base + neighbour, 0), face_index ^ 1].astype(jnp.float32)
        face_sum = face_sum + jnp.where((neighbour >= 0)[:, None], face_rows, jnp.float32(0.0))
    point_device = jnp.arange(DEVICES * RPTS, dtype=jnp.int32) // RPTS
    point_grid = point_device // N_ELEM
    point_elem = point_device % N_ELEM
    source_grid = receptors[0] // DCAP
    source_rank = receptors[0] % DCAP
    donor_device = source_grid * N_ELEM + point_elem
    donor_slot = donors[(donor_device * N_GRID + point_grid) * DCAP + source_rank]
    donor_values = first_guess[donor_device * SLOTS + donor_slot].astype(jnp.float32).reshape(-1, VARS, PTS)
    basis_table = basis_weights(receptor_coords)
    fringe_values = jnp.einsum("rvp,pr->rv", donor_values, basis_table, precision=lax.Precision.HIGHEST)
    flat_index = ((point_device * SLOTS + receptors[1]) * B)[:, None] + jnp.arange(VARS, dtype=jnp.int32)[None, :] * PTS + receptors[2][:, None]
    fringe = jnp.zeros((total_slots * B,), jnp.float32).at[flat_index.reshape(-1)].add(fringe_values.reshape(-1)).reshape(total_slots, B)
    sweep_rhs = (residual.astype(jnp.float32) - face_sum + fringe).astype(jnp.bfloat16)
    sweep_owned = sweep_rhs[owned_native].reshape(DEVICES, OWN, B)
    update_owned = lax.map(apply_blocks, (precond, sweep_owned)).reshape(DEVICES * OWN, B)
    update = jnp.where(live_slots[:, None], update_owned[own_of_native], jnp.float32(0.0))
    return precond.reshape(DEVICES * OWN, B, B), update
```

```python
import functools

import jax
import jax.numpy as jnp
from jax import lax
from jax.experimental import pallas as pl
from jax.experimental.pallas import tpu as pltpu
from jax.sharding import PartitionSpec as P

F32 = jnp.float32
BF16 = jnp.bfloat16
MESH = pl.DeviceIdType.MESH
VARS = 5
SLOTS = 32
OWN = 16
GRIDS = 32
ELEMS = 4
B = 320
PTS = 64
RPTS = 128
WIRE = 800
SELF = 30
LANES = 384
NODE_PLACES = (-1.0, -0.5, 0.5, 1.0)


def offsets(i):
    step = (i // 8 + 1) % 4
    dc = 1 - (i // 4) % 2
    j = i % 4
    dy = (1 + 2 * j - j // 2) % 4
    dz = (step + 4 - dy) % 4
    return dy, dz, dc


def partner(i, grid):
    dy, dz, dc = offsets(i)
    c, z, y = grid % 2, (grid // 2) % 4, grid // 8
    return ((y + dy) % 4) * 8 + ((z + dz) % 4) * 2 + (c + dc) % 2


def sender(i, grid):
    dy, dz, dc = offsets(i)
    c, z, y = grid % 2, (grid // 2) % 4, grid // 8
    return ((y + 4 - dy) % 4) * 8 + ((z + 4 - dz) % 4) * 2 + (c + 2 - dc) % 2


def iota(shape, dim):
    return lax.broadcasted_iota(jnp.int32, shape, dim)


def dot(a, b):
    return jnp.dot(a, b, preferred_element_type=F32)


def dot_t(a, b):
    return lax.dot_general(a, b, (((1,), (1,)), ((), ())), preferred_element_type=F32)


def column(row):
    n = row.shape[1]
    same = iota((n, n), 0) == iota((n, n), 1)
    return jnp.sum(jnp.where(same, row.astype(F32), 0.0), axis=1, keepdims=True)


def one_hot(col, n):
    lanes = iota((col.shape[0], n), 1).astype(F32)
    return jnp.where(col == lanes, 1.0, 0.0)


def two_term_dot(a, b):
    high = b.astype(BF16)
    low = (b - high.astype(F32)).astype(BF16)
    return dot(a, high) + dot(a, low)


def two_term_left(a, b):
    high = a.astype(BF16)
    low = (a - high.astype(F32)).astype(BF16)
    return dot(high, b) + dot(low, b)


def invert(matrix, eye):
    full = matrix.astype(F32)
    diag = full * eye
    by_row = 1.0 / jnp.sum(diag, axis=1, keepdims=True)
    by_col = 1.0 / jnp.sum(diag, axis=0, keepdims=True)
    approx = (eye * (2.0 * by_row) - full * by_row * by_col).astype(BF16)
    for last in (False, True):
        defect = (eye - dot(matrix, approx)).astype(BF16)
        approx = (approx.astype(F32) + dot(approx, defect)).astype(BF16)
    return approx


def lagrange(position):
    terms = []
    for k in range(4):
        value = None
        for m in range(4):
            if m != k:
                factor = (position - NODE_PLACES[m]) * (1.0 / (NODE_PLACES[k] - NODE_PLACES[m]))
                value = factor if value is None else value * factor
        terms.append(value)
    return terms


def pick(which, terms):
    return jnp.where(
        which == 0, terms[0], jnp.where(which == 1, terms[1], jnp.where(which == 2, terms[2], terms[3]))
    )


def main_kernel(
    slot_of,
    jac_hbm,
    fc_hbm,
    res_ref,
    om_ref,
    nb_ref,
    don_ref,
    rec_ref,
    xyz_ref,
    arrived,
    upd_ref,
    jac,
    inv,
    wire,
    fc,
    eye_ref,
    rhs_ref,
    row_ref,
    guess_all,
    don2,
    don_send,
    don_recv,
    faces,
    jac_sem,
    fc_sem,
    own_sem,
    send_sem,
    recv_sem,
    gs_sem,
    gr_sem,
    ds_sem,
    dr_sem,
):
    grid = lax.axis_index("grid")
    elem = lax.axis_index("elem")
    jac_copy = pltpu.make_async_copy(jac_hbm, jac, jac_sem)
    jac_copy.start()
    fc_copy = pltpu.make_async_copy(fc_hbm, fc, fc_sem)
    fc_copy.start()

    barrier = pltpu.get_barrier_semaphore()
    for i in range(GRIDS):
        if i != SELF:
            pl.semaphore_signal(
                barrier, inc=1, device_id={"grid": partner(i, grid)}, device_id_type=MESH
            )
    for k in range(1, ELEMS):
        pl.semaphore_signal(
            barrier, inc=1, device_id={"elem": (elem + k) % ELEMS}, device_id_type=MESH
        )

    def block_copy(i):
        return pltpu.make_async_remote_copy(
            src_ref=wire.at[i],
            dst_ref=arrived.at[grid],
            send_sem=send_sem.at[i],
            recv_sem=recv_sem.at[i],
            device_id={"grid": partner(i, grid)},
            device_id_type=MESH,
        )

    def block_arrival(i):
        return pltpu.make_async_remote_copy(
            src_ref=wire.at[i],
            dst_ref=arrived.at[sender(i, grid)],
            send_sem=send_sem.at[i],
            recv_sem=recv_sem.at[i],
            device_id={"grid": partner(i, grid)},
            device_id_type=MESH,
        )

    def guess_copy(k, place):
        return pltpu.make_async_remote_copy(
            src_ref=guess_all.at[elem],
            dst_ref=guess_all.at[place],
            send_sem=gs_sem.at[k],
            recv_sem=gr_sem.at[k],
            device_id={"elem": (elem + k) % ELEMS},
            device_id_type=MESH,
        )

    def donor_copy(i, place):
        return pltpu.make_async_remote_copy(
            src_ref=don_send.at[pl.ds(2 * partner(i, grid), 2)],
            dst_ref=don_recv.at[pl.ds(2 * place, 2)],
            send_sem=ds_sem.at[i],
            recv_sem=dr_sem.at[i],
            device_id={"grid": partner(i, grid)},
            device_id_type=MESH,
        )

    eye_ref[...] = jnp.where(iota((B, B), 0) == iota((B, B), 1), 1.0, 0.0)

    def partner_vector(shape, dim):
        i = iota(shape, dim)
        j = i & 3
        dy = (1 + 2 * j - (j >> 1)) & 3
        dz = ((i >> 3) + 5 - dy) & 3
        dc = 1 - ((i >> 2) & 1)
        c, z, y = grid % 2, (grid // 2) % 4, grid // 8
        return (((y + dy) & 3) * 8 + ((z + dz) & 3) * 2 + ((c + dc) & 1)).astype(F32)

    owner_row = om_ref[...].astype(F32)
    owner_col = column(om_ref[...])
    to_order = jnp.where(owner_row == partner_vector((GRIDS, SLOTS), 0), 1.0, 0.0)
    to_slot = jnp.where(owner_col == partner_vector((SLOTS, GRIDS), 1), 1.0, 0.0)
    live = jnp.sum(to_order, axis=1, keepdims=True) > 0.0
    rhs_ref[...] = dot(to_order.astype(BF16), res_ref[...])

    jac_copy.wait()

    def build(i):
        matrix = jac[slot_of[i]]
        result = invert(matrix, eye_ref[...])
        inv[i] = result
        wire[i, 0:320, :] = result[:, 0:128]
        wire[i, 320:640, :] = result[:, 128:256]
        wire[i, 640:800, :] = jnp.concatenate([result[0:160, 256:320], result[160:320, 256:320]], axis=1)
        vector = rhs_ref[pl.ds(i, 1), :].astype(BF16)
        row_ref[pl.ds(i, 1), :] = dot_t(vector, result)

    build(0)
    build(1)
    pl.semaphore_wait(barrier, GRIDS - 1 + ELEMS - 1)

    def build_step(t, carry):
        build(2 * t)
        build(2 * t + 1)

        @pl.when(t < 5)
        def _():
            block_copy(t - 1).start()

        @pl.when(jnp.logical_and(t >= 5, t % 3 != 0))
        def _():
            block_copy((t - 5) - (t - 3) // 3 + 4).start()

        return carry

    lax.fori_loop(1, 16, build_step, 0)

    guess = dot(to_slot.astype(BF16), jnp.where(live, row_ref[...], 0.0).astype(BF16)).astype(BF16)
    guess_all[elem] = guess
    donor_rows = one_hot(column(don_ref[...]), SLOTS).astype(BF16)
    don2[:, 0:B] = dot(donor_rows, guess)

    def spread(r, carry):
        don_send[r] = don2[pl.ds(r, 1), :]
        return carry

    lax.fori_loop(0, 2 * GRIDS, spread, 0, unroll=8)
    for k in range(1, ELEMS):
        guess_copy(k, elem).start()

    def start_donors(i, carry):
        @pl.when(i != SELF)
        def _():
            donor_copy(i, grid).start()

        return carry

    lax.fori_loop(0, GRIDS, start_donors, 0)

    def start_blocks(i, carry):
        @pl.when(i != SELF)
        def _():
            block_copy(i).start()

        return carry

    lax.fori_loop(11, GRIDS, start_blocks, 0)
    own_copy = pltpu.make_async_copy(wire.at[SELF], arrived.at[grid], own_sem)
    own_copy.start()

    lane = iota((RPTS, B), 1)
    point = lane & (PTS - 1)
    xs = lagrange(column(xyz_ref[0:1, :]))
    ys = lagrange(column(xyz_ref[1:2, :]))
    zs = lagrange(column(xyz_ref[2:3, :]))
    basis = pick(point >> 4, xs) * pick((point >> 2) & 3, ys) * pick(point & 3, zs)
    at_point = point.astype(F32) == column(rec_ref[2:3, :])
    donor_pick = one_hot(column(rec_ref[0:1, :]), 2 * GRIDS).astype(BF16)
    target = jnp.where(
        rec_ref[1:2, :].astype(F32) == iota((SLOTS, RPTS), 0).astype(F32), 1.0, 0.0
    ).astype(BF16)
    same_var = jnp.where((iota((B, B), 0) >> 6) == (iota((B, B), 1) >> 6), 1.0, 0.0).astype(BF16)
    face_pick = jnp.concatenate(
        [one_hot(column(nb_ref[f : f + 1, :]), ELEMS * SLOTS) for f in range(6)], axis=0
    ).astype(BF16)

    fc_copy.wait()
    for k in range(1, ELEMS):
        guess_copy(k, (elem + ELEMS - k) % ELEMS).wait()
    rows = dot(face_pick, guess_all[...].reshape(ELEMS * SLOTS, B)).astype(BF16)
    faces[...] = dot(rows, fc[...])
    face_sum = jnp.zeros((SLOTS, B), F32)
    for f in range(6):
        opposite = f ^ 1
        part = faces[f * SLOTS : (f + 1) * SLOTS, opposite * B : (opposite + 1) * B]
        face_sum = face_sum + part.astype(BF16).astype(F32)

    def wait_donors(i, carry):
        @pl.when(i != SELF)
        def _():
            donor_copy(i, sender(i, grid)).wait()

        return carry

    lax.fori_loop(0, GRIDS, wait_donors, 0)

    def collect(r, carry):
        don2[pl.ds(r, 1), :] = don_recv[r]
        return carry

    lax.fori_loop(0, 2 * GRIDS, collect, 0, unroll=8)
    mine = (iota((2 * GRIDS, B), 0) >> 1) == grid
    donor_values = jnp.where(mine, 0.0, don2[:, 0:B]).astype(BF16)
    picked = dot(donor_pick, donor_values)
    values = two_term_left(picked * basis, same_var)
    fringe = two_term_dot(target, jnp.where(at_point, values, 0.0))
    sweep = (res_ref[...].astype(F32) - face_sum + fringe).astype(BF16)
    rhs_ref[...] = dot(to_order.astype(BF16), sweep)

    def apply(i, carry):
        vector = rhs_ref[pl.ds(i, 1), :].astype(BF16)
        row_ref[pl.ds(i, 1), :] = dot_t(vector, inv[i])
        return carry

    lax.fori_loop(0, GRIDS, apply, 0, unroll=4)
    upd_ref[...] = jnp.dot(
        to_slot,
        jnp.where(live, row_ref[...], 0.0),
        precision=lax.Precision.HIGHEST,
        preferred_element_type=F32,
    )

    own_copy.wait()

    def finish(i, carry):
        @pl.when(i != SELF)
        def _():
            block_arrival(i).wait()

        return carry

    lax.fori_loop(0, GRIDS, finish, 0)


def place_kernel(owned, upd_ref, w0, w1, w2, w3, out_ref, upd_out):
    for k, w in enumerate((w0, w1, w2, w3)):
        out_ref[k, :, 0:128] = w[0, 0:320, :]
        out_ref[k, :, 128:256] = w[0, 320:640, :]
        out_ref[k, 0:160, 256:320] = w[0, 640:800, 0:64]
        out_ref[k, 160:320, 256:320] = w[0, 640:800, 64:128]

    @pl.when(pl.program_id(0) == 0)
    def _():
        upd_out[...] = upd_ref[...]


def shards(jacobians, residual, owner_map, owner_slot, face_coupling, neighbours, donors, receptors, coords):
    grid = lax.axis_index("grid")
    order = partner(jnp.arange(GRIDS, dtype=jnp.int32), grid)
    hits = owner_map[None, :] == order[:, None]
    slot_of = jnp.sum(jnp.where(hits, jnp.arange(SLOTS, dtype=jnp.int32)[None, :], 0), axis=1)

    vmem = pl.BlockSpec(memory_space=pltpu.VMEM)
    anywhere = pl.BlockSpec(memory_space=pl.ANY)
    arrived, update = pl.pallas_call(
        main_kernel,
        out_shape=(
            jax.ShapeDtypeStruct((GRIDS, WIRE, 128), BF16),
            jax.ShapeDtypeStruct((SLOTS, B), F32),
        ),
        in_specs=[pl.BlockSpec(memory_space=pltpu.SMEM), anywhere, anywhere] + [vmem] * 6,
        out_specs=(anywhere, vmem),
        scratch_shapes=[
            pltpu.VMEM((SLOTS, B, B), BF16),
            pltpu.VMEM((GRIDS, B, B), BF16),
            pltpu.VMEM((GRIDS, WIRE, 128), BF16),
            pltpu.VMEM((B, 6 * B), BF16),
            pltpu.VMEM((B, B), F32),
            pltpu.VMEM((GRIDS, B), F32),
            pltpu.VMEM((GRIDS, B), F32),
            pltpu.VMEM((ELEMS, SLOTS, B), BF16),
            pltpu.VMEM((2 * GRIDS, LANES), F32),
            pltpu.VMEM((2 * GRIDS, 1, LANES), F32),
            pltpu.VMEM((2 * GRIDS, 1, LANES), F32),
            pltpu.VMEM((6 * SLOTS, 6 * B), F32),
            pltpu.SemaphoreType.DMA,
            pltpu.SemaphoreType.DMA,
            pltpu.SemaphoreType.DMA,
            pltpu.SemaphoreType.DMA((GRIDS,)),
            pltpu.SemaphoreType.DMA((GRIDS,)),
            pltpu.SemaphoreType.DMA((ELEMS,)),
            pltpu.SemaphoreType.DMA((ELEMS,)),
            pltpu.SemaphoreType.DMA((GRIDS,)),
            pltpu.SemaphoreType.DMA((GRIDS,)),
        ],
        compiler_params=pltpu.CompilerParams(
            collective_id=0, has_side_effects=True, vmem_limit_bytes=60 * 2**20
        ),
        name="invert_send_sweep",
    )(
        slot_of,
        jacobians,
        face_coupling,
        residual,
        owner_map.reshape(1, SLOTS),
        neighbours,
        donors.reshape(1, 2 * GRIDS),
        receptors,
        coords,
    )

    def block(k):
        return pl.BlockSpec((1, WIRE, 128), lambda o, owned: (owned[4 * o + k], 0, 0))

    return pl.pallas_call(
        place_kernel,
        out_shape=(
            jax.ShapeDtypeStruct((OWN, B, B), BF16),
            jax.ShapeDtypeStruct((SLOTS, B), F32),
        ),
        grid_spec=pltpu.PrefetchScalarGridSpec(
            num_scalar_prefetch=1,
            grid=(OWN // 4,),
            in_specs=[pl.BlockSpec((SLOTS, B), lambda o, owned: (0, 0))] + [block(k) for k in range(4)],
            out_specs=(
                pl.BlockSpec((4, B, B), lambda o, owned: (o, 0, 0)),
                pl.BlockSpec((SLOTS, B), lambda o, owned: (0, 0)),
            ),
        ),
        name="place_owned",
    )(owner_slot, update, arrived, arrived, arrived, arrived)


def solution(mesh):
    in_specs = (
        P(("grid", "elem"), None, None),
        P(("grid", "elem"), None),
        P(("grid", "elem")),
        P(("grid", "elem")),
        P(),
        P(None, ("grid", "elem")),
        P(("grid", "elem")),
        P(None, ("grid", "elem")),
        P(None, ("grid", "elem")),
    )
    out_specs = (P(("grid", "elem"), None, None), P(("grid", "elem"), None))
    return jax.shard_map(shards, mesh=mesh, in_specs=in_specs, out_specs=out_specs, check_vma=False)
```

```python
import functools

import jax
import jax.numpy as jnp
from jax import lax
from jax.experimental import pallas as pl
from jax.experimental.pallas import tpu as pltpu
from jax.sharding import PartitionSpec as P

F32 = jnp.float32
BF16 = jnp.bfloat16
MESH = pl.DeviceIdType.MESH
VARS = 5
SLOTS = 32
OWN = 16
GRIDS = 32
ELEMS = 4
B = 320
PTS = 64
RPTS = 128
HEAD = 640
TAIL = 160
WIRE = HEAD + TAIL
PACK = 16
SELF = 2
GROUP = 4
TOGETHER = 4
EARLY = 4
FIRST = 2
LANES = 384
NODE_PLACES = (-1.0, -0.5, 0.5, 1.0)


def offsets(i):
    step = i // 8
    dc = (i // 4) % 2
    j = i % 4
    dy = (1 + 2 * j - j // 2) % 4
    dz = (step + 4 - dy) % 4
    return dy, dz, dc


def partner(i, grid):
    dy, dz, dc = offsets(i)
    c, z, y = grid % 2, (grid // 2) % 4, grid // 8
    return ((y + dy) % 4) * 8 + ((z + dz) % 4) * 2 + (c + dc) % 2


def sender(i, grid):
    dy, dz, dc = offsets(i)
    c, z, y = grid % 2, (grid // 2) % 4, grid // 8
    return ((y + 4 - dy) % 4) * 8 + ((z + 4 - dz) % 4) * 2 + (c + 2 - dc) % 2


def iota(shape, dim):
    return lax.broadcasted_iota(jnp.int32, shape, dim)


def dot(a, b):
    return jnp.dot(a, b, preferred_element_type=F32)


def dot_t(a, b):
    return lax.dot_general(a, b, (((1,), (1,)), ((), ())), preferred_element_type=F32)


def column(row):
    n = row.shape[1]
    same = iota((n, n), 0) == iota((n, n), 1)
    return jnp.sum(jnp.where(same, row.astype(F32), 0.0), axis=1, keepdims=True)


def one_hot(col, n):
    lanes = iota((col.shape[0], n), 1).astype(F32)
    return jnp.where(col == lanes, 1.0, 0.0)


def two_term_dot(a, b):
    high = b.astype(BF16)
    low = (b - high.astype(F32)).astype(BF16)
    return dot(a, high) + dot(a, low)


def two_term_left(a, b):
    high = a.astype(BF16)
    low = (a - high.astype(F32)).astype(BF16)
    return dot(high, b) + dot(low, b)


def scaled_start(matrix, eye):
    full = matrix.astype(F32)
    diag = full * eye
    by_row = 1.0 / jnp.sum(diag, axis=1, keepdims=True)
    by_col = 1.0 / jnp.sum(diag, axis=0, keepdims=True)
    return (eye * (2.0 * by_row) - full * by_row * by_col).astype(BF16)


def invert(matrices, eye):
    approx = [scaled_start(m, eye) for m in matrices]
    for step in range(2):
        defect = [(eye - dot(m, x)).astype(BF16) for m, x in zip(matrices, approx)]
        approx = [(x.astype(F32) + dot(x, d)).astype(BF16) for x, d in zip(approx, defect)]
    return approx


def lagrange(position):
    terms = []
    for k in range(4):
        value = None
        for m in range(4):
            if m != k:
                factor = (position - NODE_PLACES[m]) * (1.0 / (NODE_PLACES[k] - NODE_PLACES[m]))
                value = factor if value is None else value * factor
        terms.append(value)
    return terms


def pick(which, terms):
    return jnp.where(
        which == 0, terms[0], jnp.where(which == 1, terms[1], jnp.where(which == 2, terms[2], terms[3]))
    )


def main_kernel(
    jac_hbm,
    fc_hbm,
    om1_hbm,
    res_hbm,
    om_hbm,
    nb_hbm,
    don_hbm,
    rec_hbm,
    xyz_hbm,
    arrived,
    upd_hbm,
    owner_map,
    res_ref,
    om_ref,
    nb_ref,
    don_ref,
    rec_ref,
    xyz_ref,
    upd_ref,
    jac,
    inv,
    wire,
    fc,
    eye_ref,
    rhs_ref,
    acc_ref,
    guess_all,
    tails,
    faces,
    jac_sem,
    fc_sem,
    in_sem,
    upd_sem,
    own_sem,
    tails_sem,
    hs_sem,
    hr_sem,
    gs_sem,
    gr_sem,
    ts_sem,
    tr_sem,
):
    grid = lax.axis_index("grid")
    elem = lax.axis_index("elem")
    barrier = pltpu.get_barrier_semaphore()
    for i in range(GRIDS):
        if i != SELF:
            pl.semaphore_signal(
                barrier, inc=1, device_id={"grid": partner(i, grid)}, device_id_type=MESH
            )
    for k in range(1, ELEMS):
        pl.semaphore_signal(
            barrier, inc=1, device_id={"elem": (elem + k) % ELEMS}, device_id_type=MESH
        )

    small = ((om1_hbm, owner_map), (om_hbm, om_ref), (res_hbm, res_ref), (nb_hbm, nb_ref))
    small += ((don_hbm, don_ref), (rec_hbm, rec_ref), (xyz_hbm, xyz_ref))
    small_copies = [pltpu.make_async_copy(a, b, in_sem.at[k]) for k, (a, b) in enumerate(small)]
    for copy in small_copies:
        copy.start()
    jac_copy = pltpu.make_async_copy(jac_hbm, jac, jac_sem)
    jac_copy.start()
    fc_copy = pltpu.make_async_copy(fc_hbm, fc, fc_sem)
    fc_copy.start()

    def head_copy(i, place):
        return pltpu.make_async_remote_copy(
            src_ref=wire.at[i, pl.ds(0, HEAD)],
            dst_ref=arrived.at[place, pl.ds(0, HEAD)],
            send_sem=hs_sem.at[i],
            recv_sem=hr_sem.at[i],
            device_id={"grid": partner(i, grid)},
            device_id_type=MESH,
        )

    def tail_copy(i, place):
        return pltpu.make_async_remote_copy(
            src_ref=wire.at[i, pl.ds(HEAD, TAIL + PACK)],
            dst_ref=tails.at[place],
            send_sem=ts_sem.at[i],
            recv_sem=tr_sem.at[i],
            device_id={"grid": partner(i, grid)},
            device_id_type=MESH,
        )

    def guess_copy(k, place):
        return pltpu.make_async_remote_copy(
            src_ref=guess_all.at[elem],
            dst_ref=guess_all.at[place],
            send_sem=gs_sem.at[k],
            recv_sem=gr_sem.at[k],
            device_id={"elem": (elem + k) % ELEMS},
            device_id_type=MESH,
        )

    eye_ref[...] = jnp.where(iota((B, B), 0) == iota((B, B), 1), 1.0, 0.0)

    def partner_vector(i):
        j = i & 3
        dy = (1 + 2 * j - (j >> 1)) & 3
        dz = ((i >> 3) + 4 - dy) & 3
        dc = (i >> 2) & 1
        c, z, y = grid % 2, (grid // 2) % 4, grid // 8
        return (((y + dy) & 3) * 8 + ((z + dz) & 3) * 2 + ((c + dc) & 1)).astype(F32)

    for copy in small_copies:
        copy.wait()
    owner_row = om_ref[...].astype(F32)
    owner_col = column(om_ref[...])
    to_order = jnp.where(
        jnp.logical_and(owner_row == partner_vector(iota((128, SLOTS), 0)), iota((128, SLOTS), 0) < GRIDS), 1.0, 0.0
    )
    to_slot = jnp.where(
        jnp.logical_and(owner_col == partner_vector(iota((SLOTS, 128), 1)), iota((SLOTS, 128), 1) < GRIDS), 1.0, 0.0
    )
    live = jnp.sum(to_slot, axis=0, keepdims=True) > 0.0

    pack_row = iota((GRIDS * PACK, 2 * GRIDS), 0)
    pack_slot = pack_row & (PACK - 1)
    pack_kind = jnp.where(pack_slot >= 3, 1.0, 0.0)
    wanted_entry = 2.0 * partner_vector(pack_row >> 4) + pack_kind
    entry_lane = iota((GRIDS * PACK, 2 * GRIDS), 1).astype(F32)
    entries = jnp.where(wanted_entry == entry_lane, don_ref[...].astype(F32), 0.0)
    entry = jnp.sum(entries, axis=1, keepdims=True)
    used = (iota((GRIDS * PACK, SLOTS), 0) & (PACK - 1)) < 6
    donor_rows = jnp.where(used, one_hot(entry, SLOTS), 0.0).astype(BF16)

    def ordered_columns(rows):
        ordered = dot(to_order.astype(BF16), rows).astype(BF16)
        return dot_t(eye_ref[...].astype(BF16), ordered).astype(BF16)

    rhs_ref[...] = ordered_columns(res_ref[...])
    acc_ref[...] = jnp.zeros((B, 128), F32)

    jac_copy.wait()

    def slot_of(i):
        wanted = partner(i, grid)
        slot = jnp.int32(0)
        for k in range(SLOTS):
            slot = jnp.where(owner_map[k] == wanted, jnp.int32(k), slot)
        return slot

    order_lane = iota((B, 128), 1)

    def build(first, count):
        places = [first + k for k in range(count)]
        results = invert([jac[slot_of(i)] for i in places], eye_ref[...])
        for i, result in zip(places, results):
            inv[i] = result
            wire[i, 0:320, :] = result[:, 0:128]
            wire[i, 320:640, :] = result[:, 128:256]
            wire[i, HEAD:WIRE, :] = jnp.concatenate([result[0:160, 256:320], result[160:320, 256:320]], axis=1)
        products = [dot(result, rhs_ref[...]) for result in results]
        total = acc_ref[...]
        for i, product in zip(places, products):
            total = jnp.where(order_lane == i, product, total)
        acc_ref[...] = total

    def build_group(q):
        for k in range(0, GROUP, TOGETHER):
            build(GROUP * q + k, TOGETHER)

    def send_group(q):
        for k in range(GROUP):
            if isinstance(q, int) and GROUP * q + k == SELF:
                continue
            head_copy(GROUP * q + k, grid).start()

    def build_first(q, carry):
        build_group(q)
        return carry

    lax.fori_loop(0, 2, build_first, 0)
    pl.semaphore_wait(barrier, GRIDS - 1 + ELEMS - 1)
    for q in range(FIRST):
        send_group(q)

    def build_next(q, carry):
        build_group(q)

        @pl.when(jnp.logical_and(q % 2 == 0, q >= 4))
        def _():
            send_group(q // 2)

        return carry

    lax.fori_loop(2, GRIDS // GROUP, build_next, 0)

    guess = dot_t(to_slot.astype(BF16), jnp.where(live, acc_ref[...], 0.0).astype(BF16)).astype(BF16)
    guess_all[elem] = guess
    for k in range(1, ELEMS):
        guess_copy(k, elem).start()
    wide = jnp.concatenate([guess, jnp.zeros((SLOTS, LANES - B), BF16)], axis=1)
    spread = dot(donor_rows, wide)
    row = iota((GRIDS * PACK, 128), 0) & (PACK - 1)
    third = jnp.where(row >= 3, row - 3, row)
    packed = jnp.where(
        third == 0, spread[:, 0:128], jnp.where(third == 1, spread[:, 128:256], spread[:, 256:384])
    )
    wire[:, WIRE : WIRE + PACK, :] = packed.astype(BF16).reshape(GRIDS, PACK, 128)
    tails[grid] = wire[SELF, HEAD : WIRE + PACK, :]

    def send_tails(i, carry):
        @pl.when(i != SELF)
        def _():
            tail_copy(i, grid).start()

        return carry

    lax.fori_loop(0, GRIDS, send_tails, 0)

    def send_rest(q, carry):
        send_group(q)
        return carry

    lax.fori_loop(EARLY, GRIDS // GROUP, send_rest, 0)
    own_copy = pltpu.make_async_copy(wire.at[SELF, pl.ds(0, HEAD)], arrived.at[grid, pl.ds(0, HEAD)], own_sem)
    own_copy.start()

    lane = iota((RPTS, B), 1)
    point = lane & (PTS - 1)
    xs = lagrange(column(xyz_ref[0:1, :]))
    ys = lagrange(column(xyz_ref[1:2, :]))
    zs = lagrange(column(xyz_ref[2:3, :]))
    basis = pick(point >> 4, xs) * pick((point >> 2) & 3, ys) * pick(point & 3, zs)
    at_point = point.astype(F32) == column(rec_ref[2:3, :])
    donor_col = column(rec_ref[0:1, :])
    donor_grid = jnp.floor(donor_col * 0.5)
    donor_base = PACK * donor_grid + 3.0 * (donor_col - 2.0 * donor_grid)
    target = jnp.where(
        rec_ref[1:2, :].astype(F32) == iota((SLOTS, RPTS), 0).astype(F32), 1.0, 0.0
    ).astype(BF16)
    same_var = jnp.where((iota((B, B), 0) >> 6) == (iota((B, B), 1) >> 6), 1.0, 0.0).astype(BF16)
    face_pick = jnp.concatenate(
        [one_hot(column(nb_ref[f : f + 1, :]), ELEMS * SLOTS) for f in range(6)], axis=0
    ).astype(BF16)

    fc_copy.wait()
    for k in range(1, ELEMS):
        guess_copy(k, (elem + ELEMS - k) % ELEMS).wait()
    rows = dot(face_pick, guess_all[...].reshape(ELEMS * SLOTS, B)).astype(BF16)
    faces[...] = dot(rows, fc[...])
    face_sum = jnp.zeros((SLOTS, B), F32)
    for f in range(6):
        opposite = f ^ 1
        part = faces[f * SLOTS : (f + 1) * SLOTS, opposite * B : (opposite + 1) * B]
        face_sum = face_sum + part.astype(BF16).astype(F32)

    def wait_tails(i, carry):
        @pl.when(i != SELF)
        def _():
            tail_copy(i, sender(i, grid)).wait()

        return carry

    lax.fori_loop(0, GRIDS, wait_tails, 0)
    tails_copy = pltpu.make_async_copy(
        tails.at[:, pl.ds(0, TAIL)], arrived.at[:, pl.ds(HEAD, TAIL)], tails_sem
    )
    tails_copy.start()
    packs = tails[:, TAIL : TAIL + PACK, :].reshape(GRIDS * PACK, 128)
    picked = jnp.concatenate(
        [dot(one_hot(donor_base + float(q), GRIDS * PACK).astype(BF16), packs) for q in range(3)], axis=1
    )[:, 0:B]
    values = two_term_left(picked * basis, same_var)
    fringe = two_term_dot(target, jnp.where(at_point, values, 0.0))
    sweep = (res_ref[...].astype(F32) - face_sum + fringe).astype(BF16)
    rhs_ref[...] = ordered_columns(sweep)

    def apply(q, carry):
        places = [GROUP * q + k for k in range(GROUP)]
        products = [dot(inv[i], rhs_ref[...]) for i in places]
        total = acc_ref[...]
        for i, product in zip(places, products):
            total = jnp.where(order_lane == i, product, total)
        acc_ref[...] = total
        return carry

    lax.fori_loop(0, GRIDS // GROUP, apply, 0)
    upd_ref[...] = lax.dot_general(
        to_slot,
        jnp.where(live, acc_ref[...], 0.0),
        (((1,), (1,)), ((), ())),
        precision=lax.Precision.HIGHEST,
        preferred_element_type=F32,
    )
    upd_copy = pltpu.make_async_copy(upd_ref, upd_hbm, upd_sem)
    upd_copy.start()
    own_copy.wait()
    upd_copy.wait()

    tails_copy.wait()

    def finish(i, carry):
        @pl.when(i != SELF)
        def _():
            head_copy(i, sender(i, grid)).wait()

        return carry

    lax.fori_loop(0, GRIDS, finish, 0)


def place_kernel(owned, upd_ref, w0, w1, w2, w3, out_ref, upd_out):
    for k, w in enumerate((w0, w1, w2, w3)):
        out_ref[k, :, 0:128] = w[0, 0:320, :]
        out_ref[k, :, 128:256] = w[0, 320:640, :]
        out_ref[k, 0:160, 256:320] = w[0, 640:800, 0:64]
        out_ref[k, 160:320, 256:320] = w[0, 640:800, 64:128]

    @pl.when(pl.program_id(0) == 0)
    def _():
        upd_out[...] = upd_ref[...]


def shards(jacobians, residual, owner_map, owner_slot, face_coupling, neighbours, donors, receptors, coords):
    anywhere = pl.BlockSpec(memory_space=pl.ANY)
    arrived, update = pl.pallas_call(
        main_kernel,
        out_shape=(
            jax.ShapeDtypeStruct((GRIDS, WIRE, 128), BF16),
            jax.ShapeDtypeStruct((SLOTS, B), F32),
        ),
        in_specs=[anywhere] * 9,
        out_specs=(anywhere, anywhere),
        scratch_shapes=[
            pltpu.SMEM((SLOTS,), jnp.int32),
            pltpu.VMEM((SLOTS, B), BF16),
            pltpu.VMEM((1, SLOTS), jnp.int32),
            pltpu.VMEM((6, SLOTS), jnp.int32),
            pltpu.VMEM((1, 2 * GRIDS), jnp.int32),
            pltpu.VMEM((3, RPTS), jnp.int32),
            pltpu.VMEM((3, RPTS), F32),
            pltpu.VMEM((SLOTS, B), F32),
            pltpu.VMEM((SLOTS, B, B), BF16),
            pltpu.VMEM((GRIDS, B, B), BF16),
            pltpu.VMEM((GRIDS, WIRE + PACK, 128), BF16),
            pltpu.VMEM((B, 6 * B), BF16),
            pltpu.VMEM((B, B), F32),
            pltpu.VMEM((B, 128), BF16),
            pltpu.VMEM((B, 128), F32),
            pltpu.VMEM((ELEMS, SLOTS, B), BF16),
            pltpu.VMEM((GRIDS, TAIL + PACK, 128), BF16),
            pltpu.VMEM((6 * SLOTS, 6 * B), F32),
            pltpu.SemaphoreType.DMA,
            pltpu.SemaphoreType.DMA,
            pltpu.SemaphoreType.DMA((7,)),
            pltpu.SemaphoreType.DMA,
            pltpu.SemaphoreType.DMA,
            pltpu.SemaphoreType.DMA,
            pltpu.SemaphoreType.DMA((GRIDS,)),
            pltpu.SemaphoreType.DMA((GRIDS,)),
            pltpu.SemaphoreType.DMA((ELEMS,)),
            pltpu.SemaphoreType.DMA((ELEMS,)),
            pltpu.SemaphoreType.DMA((GRIDS,)),
            pltpu.SemaphoreType.DMA((GRIDS,)),
        ],
        compiler_params=pltpu.CompilerParams(
            collective_id=0, has_side_effects=True, vmem_limit_bytes=60 * 2**20
        ),
        name="invert_send_sweep",
    )(
        jacobians,
        face_coupling,
        owner_map,
        residual,
        owner_map.reshape(1, SLOTS),
        neighbours,
        donors.reshape(1, 2 * GRIDS),
        receptors,
        coords,
    )

    def block(k):
        return pl.BlockSpec((1, WIRE, 128), lambda o, owned: (owned[4 * o + k], 0, 0))

    return pl.pallas_call(
        place_kernel,
        out_shape=(
            jax.ShapeDtypeStruct((OWN, B, B), BF16),
            jax.ShapeDtypeStruct((SLOTS, B), F32),
        ),
        grid_spec=pltpu.PrefetchScalarGridSpec(
            num_scalar_prefetch=1,
            grid=(OWN // 4,),
            in_specs=[pl.BlockSpec((SLOTS, B), lambda o, owned: (0, 0))] + [block(k) for k in range(4)],
            out_specs=(
                pl.BlockSpec((4, B, B), lambda o, owned: (o, 0, 0)),
                pl.BlockSpec((SLOTS, B), lambda o, owned: (0, 0)),
            ),
        ),
        name="place_owned",
    )(owner_slot, update, arrived, arrived, arrived, arrived)


def solution(mesh):
    in_specs = (
        P(("grid", "elem"), None, None),
        P(("grid", "elem"), None),
        P(("grid", "elem")),
        P(("grid", "elem")),
        P(),
        P(None, ("grid", "elem")),
        P(("grid", "elem")),
        P(None, ("grid", "elem")),
        P(None, ("grid", "elem")),
    )
    out_specs = (P(("grid", "elem"), None, None), P(("grid", "elem"), None))
    return jax.shard_map(shards, mesh=mesh, in_specs=in_specs, out_specs=out_specs, check_vma=False)
```

```python
import functools

import jax
import jax.numpy as jnp
from jax import lax
from jax.experimental import pallas as pl
from jax.experimental.pallas import tpu as pltpu
from jax.sharding import PartitionSpec as P

F32 = jnp.float32
BF16 = jnp.bfloat16
MESH = pl.DeviceIdType.MESH
VARS = 5
SLOTS = 32
OWN = 16
GRIDS = 32
ELEMS = 4
B = 320
PTS = 64
RPTS = 128
HEAD = 640
TAIL = 160
WIRE = HEAD + TAIL
PACK = 16
HALVES = 2
SELF = 2
GROUP = 4
TOGETHER = 4
EARLY = 4
LANES = 384
NODE_PLACES = (-1.0, -0.5, 0.5, 1.0)


def offsets(i):
    step = i // 8
    dc = (i // 4) % 2
    j = i % 4
    dy = (1 + 2 * j - j // 2) % 4
    dz = (step + 4 - dy) % 4
    return dy, dz, dc


def partner(i, grid):
    dy, dz, dc = offsets(i)
    c, z, y = grid % 2, (grid // 2) % 4, grid // 8
    return ((y + dy) % 4) * 8 + ((z + dz) % 4) * 2 + (c + dc) % 2


def sender(i, grid):
    dy, dz, dc = offsets(i)
    c, z, y = grid % 2, (grid // 2) % 4, grid // 8
    return ((y + 4 - dy) % 4) * 8 + ((z + 4 - dz) % 4) * 2 + (c + 2 - dc) % 2


def iota(shape, dim):
    return lax.broadcasted_iota(jnp.int32, shape, dim)


def dot(a, b):
    return jnp.dot(a, b, preferred_element_type=F32)


def dot_t(a, b):
    return lax.dot_general(a, b, (((1,), (1,)), ((), ())), preferred_element_type=F32)


def column(row):
    n = row.shape[1]
    same = iota((n, n), 0) == iota((n, n), 1)
    return jnp.sum(jnp.where(same, row.astype(F32), 0.0), axis=1, keepdims=True)


def one_hot(col, n):
    lanes = iota((col.shape[0], n), 1).astype(F32)
    return jnp.where(col == lanes, 1.0, 0.0)


def two_term_dot(a, b):
    high = b.astype(BF16)
    low = (b - high.astype(F32)).astype(BF16)
    return dot(a, high) + dot(a, low)


def two_term_left(a, b):
    high = a.astype(BF16)
    low = (a - high.astype(F32)).astype(BF16)
    return dot(high, b) + dot(low, b)


def scaled_start(matrix, eye):
    full = matrix.astype(F32)
    diag = full * eye
    by_row = 1.0 / jnp.sum(diag, axis=1, keepdims=True)
    by_col = 1.0 / jnp.sum(diag, axis=0, keepdims=True)
    return (eye * (2.0 * by_row) - full * by_row * by_col).astype(BF16)


def invert(matrices, eye):
    approx = [scaled_start(m, eye) for m in matrices]
    for step in range(2):
        defect = [(eye - dot(m, x)).astype(BF16) for m, x in zip(matrices, approx)]
        approx = [(x.astype(F32) + dot(x, d)).astype(BF16) for x, d in zip(approx, defect)]
    return approx


def lagrange(position):
    terms = []
    for k in range(4):
        value = None
        for m in range(4):
            if m != k:
                factor = (position - NODE_PLACES[m]) * (1.0 / (NODE_PLACES[k] - NODE_PLACES[m]))
                value = factor if value is None else value * factor
        terms.append(value)
    return terms


def pick(which, terms):
    return jnp.where(
        which == 0, terms[0], jnp.where(which == 1, terms[1], jnp.where(which == 2, terms[2], terms[3]))
    )


def main_kernel(
    jac_hbm,
    fc_hbm,
    om1_hbm,
    res_hbm,
    om_hbm,
    nb_hbm,
    don_hbm,
    rec_hbm,
    xyz_hbm,
    arrived,
    upd_hbm,
    owner_map,
    res_ref,
    om_ref,
    nb_ref,
    don_ref,
    rec_ref,
    xyz_ref,
    upd_ref,
    jac,
    inv,
    wire,
    fc,
    eye_ref,
    rhs_ref,
    acc_ref,
    guess_all,
    tails,
    faces,
    jac_sem,
    fc_sem,
    in_sem,
    upd_sem,
    own_sem,
    tails_sem,
    hs_sem,
    hr_sem,
    gs_sem,
    gr_sem,
    ts_sem,
    tr_sem,
):
    grid = lax.axis_index("grid")
    elem = lax.axis_index("elem")
    barrier = pltpu.get_barrier_semaphore()
    for i in range(GRIDS):
        if i != SELF:
            pl.semaphore_signal(
                barrier, inc=1, device_id={"grid": partner(i, grid)}, device_id_type=MESH
            )
    for k in range(1, ELEMS):
        pl.semaphore_signal(
            barrier, inc=1, device_id={"elem": (elem + k) % ELEMS}, device_id_type=MESH
        )

    small = ((om1_hbm, owner_map), (om_hbm, om_ref), (res_hbm, res_ref), (nb_hbm, nb_ref))
    small += ((don_hbm, don_ref), (rec_hbm, rec_ref), (xyz_hbm, xyz_ref))
    small_copies = [pltpu.make_async_copy(a, b, in_sem.at[k]) for k, (a, b) in enumerate(small)]
    for copy in small_copies:
        copy.start()
    jac_copy = pltpu.make_async_copy(jac_hbm, jac, jac_sem)
    jac_copy.start()
    fc_copy = pltpu.make_async_copy(fc_hbm, fc, fc_sem)
    fc_copy.start()

    def head_copy(i, h, place):
        rows = pl.ds(h * (HEAD // HALVES), HEAD // HALVES)
        return pltpu.make_async_remote_copy(
            src_ref=wire.at[i, rows],
            dst_ref=arrived.at[place, rows],
            send_sem=hs_sem.at[i, h],
            recv_sem=hr_sem.at[i, h],
            device_id={"grid": partner(i, grid)},
            device_id_type=MESH,
        )

    def tail_copy(i, place):
        return pltpu.make_async_remote_copy(
            src_ref=wire.at[i, pl.ds(HEAD, TAIL + PACK)],
            dst_ref=tails.at[place],
            send_sem=ts_sem.at[i],
            recv_sem=tr_sem.at[i],
            device_id={"grid": partner(i, grid)},
            device_id_type=MESH,
        )

    def guess_copy(k, place):
        return pltpu.make_async_remote_copy(
            src_ref=guess_all.at[elem],
            dst_ref=guess_all.at[place],
            send_sem=gs_sem.at[k],
            recv_sem=gr_sem.at[k],
            device_id={"elem": (elem + k) % ELEMS},
            device_id_type=MESH,
        )

    eye_ref[...] = jnp.where(iota((B, B), 0) == iota((B, B), 1), 1.0, 0.0)

    def partner_vector(i):
        j = i & 3
        dy = (1 + 2 * j - (j >> 1)) & 3
        dz = ((i >> 3) + 4 - dy) & 3
        dc = (i >> 2) & 1
        c, z, y = grid % 2, (grid // 2) % 4, grid // 8
        return (((y + dy) & 3) * 8 + ((z + dz) & 3) * 2 + ((c + dc) & 1)).astype(F32)

    for copy in small_copies:
        copy.wait()
    owner_row = om_ref[...].astype(F32)
    owner_col = column(om_ref[...])
    to_order = jnp.where(
        jnp.logical_and(owner_row == partner_vector(iota((128, SLOTS), 0)), iota((128, SLOTS), 0) < GRIDS), 1.0, 0.0
    )
    to_slot = jnp.where(
        jnp.logical_and(owner_col == partner_vector(iota((SLOTS, 128), 1)), iota((SLOTS, 128), 1) < GRIDS), 1.0, 0.0
    )
    live = jnp.sum(to_slot, axis=0, keepdims=True) > 0.0

    def ordered_columns(rows):
        ordered = dot(to_order.astype(BF16), rows).astype(BF16)
        return dot_t(eye_ref[...].astype(BF16), ordered).astype(BF16)

    rhs_ref[...] = ordered_columns(res_ref[...])
    acc_ref[...] = jnp.zeros((B, 128), F32)

    jac_copy.wait()

    def slot_of(i):
        wanted = partner(i, grid)
        slot = jnp.int32(0)
        for k in range(SLOTS):
            slot = jnp.where(owner_map[k] == wanted, jnp.int32(k), slot)
        return slot

    order_lane = iota((B, 128), 1)

    def build(first, count):
        places = [first + k for k in range(count)]
        results = invert([jac[slot_of(i)] for i in places], eye_ref[...])
        for i, result in zip(places, results):
            inv[i] = result
            wire[i, 0:320, :] = result[:, 0:128]
            wire[i, 320:640, :] = result[:, 128:256]
            wire[i, HEAD:WIRE, :] = jnp.concatenate([result[0:160, 256:320], result[160:320, 256:320]], axis=1)
        products = [dot(result, rhs_ref[...]) for result in results]
        total = acc_ref[...]
        for i, product in zip(places, products):
            total = jnp.where(order_lane == i, product, total)
        acc_ref[...] = total

    def build_group(q):
        for k in range(0, GROUP, TOGETHER):
            build(GROUP * q + k, TOGETHER)

    def send_half(q, h):
        for k in range(GROUP):
            if isinstance(q, int) and GROUP * q + k == SELF:
                continue
            head_copy(GROUP * q + k, h, grid).start()

    def send_group(q):
        for h in range(HALVES):
            send_half(q, h)

    build_group(0)
    pl.semaphore_wait(barrier, GRIDS - 1 + ELEMS - 1)
    send_group(0)

    def build_next(q, carry):
        build_group(q)

        @pl.when(q < 3)
        def _():
            send_group(q)

        @pl.when(q == 5)
        def _():
            send_group(3)

        return carry

    lax.fori_loop(1, GRIDS // GROUP, build_next, 0)

    guess = dot_t(to_slot.astype(BF16), jnp.where(live, acc_ref[...], 0.0).astype(BF16)).astype(BF16)
    guess_all[elem] = guess
    for k in range(1, ELEMS):
        guess_copy(k, elem).start()
    pack_row = iota((GRIDS * PACK, 2 * GRIDS), 0)
    pack_slot = pack_row & (PACK - 1)
    pack_kind = jnp.where(pack_slot >= 3, 1.0, 0.0)
    wanted_entry = 2.0 * partner_vector(pack_row >> 4) + pack_kind
    entry_lane = iota((GRIDS * PACK, 2 * GRIDS), 1).astype(F32)
    entries = jnp.where(wanted_entry == entry_lane, don_ref[...].astype(F32), 0.0)
    entry = jnp.sum(entries, axis=1, keepdims=True)
    used = (iota((GRIDS * PACK, SLOTS), 0) & (PACK - 1)) < 6
    donor_rows = jnp.where(used, one_hot(entry, SLOTS), 0.0).astype(BF16)
    wide = jnp.concatenate([guess, jnp.zeros((SLOTS, LANES - B), BF16)], axis=1)
    spread = dot(donor_rows, wide)
    row = iota((GRIDS * PACK, 128), 0) & (PACK - 1)
    third = jnp.where(row >= 3, row - 3, row)
    packed = jnp.where(
        third == 0, spread[:, 0:128], jnp.where(third == 1, spread[:, 128:256], spread[:, 256:384])
    )
    wire[:, WIRE : WIRE + PACK, :] = packed.astype(BF16).reshape(GRIDS, PACK, 128)
    tails[grid] = wire[SELF, HEAD : WIRE + PACK, :]

    def send_tails(i, carry):
        @pl.when(i != SELF)
        def _():
            tail_copy(i, grid).start()

        return carry

    lax.fori_loop(0, GRIDS, send_tails, 0)

    for h in range(HALVES):

        def send_rest(q, carry, h=h):
            send_half(q, h)
            return carry

        lax.fori_loop(EARLY, GRIDS // GROUP, send_rest, 0)
    own_copy = pltpu.make_async_copy(wire.at[SELF, pl.ds(0, HEAD)], arrived.at[grid, pl.ds(0, HEAD)], own_sem)
    own_copy.start()

    lane = iota((RPTS, B), 1)
    point = lane & (PTS - 1)
    xs = lagrange(column(xyz_ref[0:1, :]))
    ys = lagrange(column(xyz_ref[1:2, :]))
    zs = lagrange(column(xyz_ref[2:3, :]))
    basis = pick(point >> 4, xs) * pick((point >> 2) & 3, ys) * pick(point & 3, zs)
    at_point = point.astype(F32) == column(rec_ref[2:3, :])
    donor_col = column(rec_ref[0:1, :])
    donor_grid = jnp.floor(donor_col * 0.5)
    donor_base = PACK * donor_grid + 3.0 * (donor_col - 2.0 * donor_grid)
    target = jnp.where(
        rec_ref[1:2, :].astype(F32) == iota((SLOTS, RPTS), 0).astype(F32), 1.0, 0.0
    ).astype(BF16)
    same_var = jnp.where((iota((B, B), 0) >> 6) == (iota((B, B), 1) >> 6), 1.0, 0.0).astype(BF16)
    face_pick = jnp.concatenate(
        [one_hot(column(nb_ref[f : f + 1, :]), ELEMS * SLOTS) for f in range(6)], axis=0
    ).astype(BF16)

    fc_copy.wait()
    for k in range(1, ELEMS):
        guess_copy(k, (elem + ELEMS - k) % ELEMS).wait()
    rows = dot(face_pick, guess_all[...].reshape(ELEMS * SLOTS, B)).astype(BF16)
    faces[...] = dot(rows, fc[...])
    face_sum = jnp.zeros((SLOTS, B), F32)
    for f in range(6):
        opposite = f ^ 1
        part = faces[f * SLOTS : (f + 1) * SLOTS, opposite * B : (opposite + 1) * B]
        face_sum = face_sum + part.astype(BF16).astype(F32)

    def wait_tails(i, carry):
        @pl.when(i != SELF)
        def _():
            tail_copy(i, sender(i, grid)).wait()

        return carry

    lax.fori_loop(0, GRIDS, wait_tails, 0)
    tails_copy = pltpu.make_async_copy(
        tails.at[:, pl.ds(0, TAIL)], arrived.at[:, pl.ds(HEAD, TAIL)], tails_sem
    )
    tails_copy.start()
    packs = tails[:, TAIL : TAIL + PACK, :].reshape(GRIDS * PACK, 128)
    picked = jnp.concatenate(
        [dot(one_hot(donor_base + float(q), GRIDS * PACK).astype(BF16), packs) for q in range(3)], axis=1
    )[:, 0:B]
    values = two_term_left(picked * basis, same_var)
    fringe = two_term_dot(target, jnp.where(at_point, values, 0.0))
    sweep = (res_ref[...].astype(F32) - face_sum + fringe).astype(BF16)
    rhs_ref[...] = ordered_columns(sweep)

    def apply(q, carry):
        places = [GROUP * q + k for k in range(GROUP)]
        products = [dot(inv[i], rhs_ref[...]) for i in places]
        total = acc_ref[...]
        for i, product in zip(places, products):
            total = jnp.where(order_lane == i, product, total)
        acc_ref[...] = total
        return carry

    lax.fori_loop(0, GRIDS // GROUP, apply, 0)
    upd_ref[...] = lax.dot_general(
        to_slot,
        jnp.where(live, acc_ref[...], 0.0),
        (((1,), (1,)), ((), ())),
        precision=lax.Precision.HIGHEST,
        preferred_element_type=F32,
    )
    upd_copy = pltpu.make_async_copy(upd_ref, upd_hbm, upd_sem)
    upd_copy.start()
    own_copy.wait()
    upd_copy.wait()

    tails_copy.wait()

    def finish(i, carry):
        @pl.when(i != SELF)
        def _():
            for h in range(HALVES):
                head_copy(i, h, sender(i, grid)).wait()

        return carry

    lax.fori_loop(0, GRIDS, finish, 0)


def place_kernel(owned, upd_ref, w0, w1, w2, w3, out_ref, upd_out):
    for k, w in enumerate((w0, w1, w2, w3)):
        out_ref[k, :, 0:128] = w[0, 0:320, :]
        out_ref[k, :, 128:256] = w[0, 320:640, :]
        out_ref[k, 0:160, 256:320] = w[0, 640:800, 0:64]
        out_ref[k, 160:320, 256:320] = w[0, 640:800, 64:128]

    @pl.when(pl.program_id(0) == 0)
    def _():
        upd_out[...] = upd_ref[...]


def shards(jacobians, residual, owner_map, owner_slot, face_coupling, neighbours, donors, receptors, coords):
    anywhere = pl.BlockSpec(memory_space=pl.ANY)
    arrived, update = pl.pallas_call(
        main_kernel,
        out_shape=(
            jax.ShapeDtypeStruct((GRIDS, WIRE, 128), BF16),
            jax.ShapeDtypeStruct((SLOTS, B), F32),
        ),
        in_specs=[anywhere] * 9,
        out_specs=(anywhere, anywhere),
        scratch_shapes=[
            pltpu.SMEM((SLOTS,), jnp.int32),
            pltpu.VMEM((SLOTS, B), BF16),
            pltpu.VMEM((1, SLOTS), jnp.int32),
            pltpu.VMEM((6, SLOTS), jnp.int32),
            pltpu.VMEM((1, 2 * GRIDS), jnp.int32),
            pltpu.VMEM((3, RPTS), jnp.int32),
            pltpu.VMEM((3, RPTS), F32),
            pltpu.VMEM((SLOTS, B), F32),
            pltpu.VMEM((SLOTS, B, B), BF16),
            pltpu.VMEM((GRIDS, B, B), BF16),
            pltpu.VMEM((GRIDS, WIRE + PACK, 128), BF16),
            pltpu.VMEM((B, 6 * B), BF16),
            pltpu.VMEM((B, B), F32),
            pltpu.VMEM((B, 128), BF16),
            pltpu.VMEM((B, 128), F32),
            pltpu.VMEM((ELEMS, SLOTS, B), BF16),
            pltpu.VMEM((GRIDS, TAIL + PACK, 128), BF16),
            pltpu.VMEM((6 * SLOTS, 6 * B), F32),
            pltpu.SemaphoreType.DMA,
            pltpu.SemaphoreType.DMA,
            pltpu.SemaphoreType.DMA((7,)),
            pltpu.SemaphoreType.DMA,
            pltpu.SemaphoreType.DMA,
            pltpu.SemaphoreType.DMA,
            pltpu.SemaphoreType.DMA((GRIDS, HALVES)),
            pltpu.SemaphoreType.DMA((GRIDS, HALVES)),
            pltpu.SemaphoreType.DMA((ELEMS,)),
            pltpu.SemaphoreType.DMA((ELEMS,)),
            pltpu.SemaphoreType.DMA((GRIDS,)),
            pltpu.SemaphoreType.DMA((GRIDS,)),
        ],
        compiler_params=pltpu.CompilerParams(
            collective_id=0, has_side_effects=True, vmem_limit_bytes=60 * 2**20
        ),
        name="invert_send_sweep",
    )(
        jacobians,
        face_coupling,
        owner_map,
        residual,
        owner_map.reshape(1, SLOTS),
        neighbours,
        donors.reshape(1, 2 * GRIDS),
        receptors,
        coords,
    )

    def block(k):
        return pl.BlockSpec((1, WIRE, 128), lambda o, owned: (owned[4 * o + k], 0, 0))

    return pl.pallas_call(
        place_kernel,
        out_shape=(
            jax.ShapeDtypeStruct((OWN, B, B), BF16),
            jax.ShapeDtypeStruct((SLOTS, B), F32),
        ),
        grid_spec=pltpu.PrefetchScalarGridSpec(
            num_scalar_prefetch=1,
            grid=(OWN // 4,),
            in_specs=[pl.BlockSpec((SLOTS, B), lambda o, owned: (0, 0))] + [block(k) for k in range(4)],
            out_specs=(
                pl.BlockSpec((4, B, B), lambda o, owned: (o, 0, 0)),
                pl.BlockSpec((SLOTS, B), lambda o, owned: (0, 0)),
            ),
        ),
        name="place_owned",
    )(owner_slot, update, arrived, arrived, arrived, arrived)


def solution(mesh):
    in_specs = (
        P(("grid", "elem"), None, None),
        P(("grid", "elem"), None),
        P(("grid", "elem")),
        P(("grid", "elem")),
        P(),
        P(None, ("grid", "elem")),
        P(("grid", "elem")),
        P(None, ("grid", "elem")),
        P(None, ("grid", "elem")),
    )
    out_specs = (P(("grid", "elem"), None, None), P(("grid", "elem"), None))
    return jax.shard_map(shards, mesh=mesh, in_specs=in_specs, out_specs=out_specs, check_vma=False)
```

```python
import functools

import jax
import jax.numpy as jnp
from jax import lax
from jax.experimental import pallas as pl
from jax.experimental.pallas import tpu as pltpu
from jax.sharding import PartitionSpec as P

F32 = jnp.float32
BF16 = jnp.bfloat16
MESH = pl.DeviceIdType.MESH
VARS = 5
SLOTS = 32
OWN = 16
GRIDS = 32
ELEMS = 4
B = 320
PTS = 64
RPTS = 128
HEAD = 640
TAIL = 160
WIRE = HEAD + TAIL
PACK = 16
HALVES = 2
SELF = 26
GROUP = 4
TOGETHER = 4
EARLY = 5
LANES = 384
NODE_PLACES = (-1.0, -0.5, 0.5, 1.0)


def offsets(i):
    step = (i // 8 + 1) % 4
    dc = (i // 4) % 2
    j = i % 4
    dy = (1 + 2 * j - j // 2) % 4
    dz = (step + 4 - dy) % 4
    return dy, dz, dc


def partner(i, grid):
    dy, dz, dc = offsets(i)
    c, z, y = grid % 2, (grid // 2) % 4, grid // 8
    return ((y + dy) % 4) * 8 + ((z + dz) % 4) * 2 + (c + dc) % 2


def sender(i, grid):
    dy, dz, dc = offsets(i)
    c, z, y = grid % 2, (grid // 2) % 4, grid // 8
    return ((y + 4 - dy) % 4) * 8 + ((z + 4 - dz) % 4) * 2 + (c + 2 - dc) % 2


def iota(shape, dim):
    return lax.broadcasted_iota(jnp.int32, shape, dim)


def dot(a, b):
    return jnp.dot(a, b, preferred_element_type=F32)


def dot_t(a, b):
    return lax.dot_general(a, b, (((1,), (1,)), ((), ())), preferred_element_type=F32)


def column(row):
    n = row.shape[1]
    same = iota((n, n), 0) == iota((n, n), 1)
    return jnp.sum(jnp.where(same, row.astype(F32), 0.0), axis=1, keepdims=True)


def one_hot(col, n):
    lanes = iota((col.shape[0], n), 1).astype(F32)
    return jnp.where(col == lanes, 1.0, 0.0)


def two_term_dot(a, b):
    high = b.astype(BF16)
    low = (b - high.astype(F32)).astype(BF16)
    return dot(a, high) + dot(a, low)


def two_term_left(a, b):
    high = a.astype(BF16)
    low = (a - high.astype(F32)).astype(BF16)
    return dot(high, b) + dot(low, b)


def scaled_start(matrix, eye):
    full = matrix.astype(F32)
    diag = full * eye
    by_row = 1.0 / jnp.sum(diag, axis=1, keepdims=True)
    by_col = 1.0 / jnp.sum(diag, axis=0, keepdims=True)
    return (eye * (2.0 * by_row) - full * by_row * by_col).astype(BF16)


def invert(matrices, eye):
    approx = [scaled_start(m, eye) for m in matrices]
    for step in range(2):
        defect = [(eye - dot(m, x)).astype(BF16) for m, x in zip(matrices, approx)]
        approx = [(x.astype(F32) + dot(x, d)).astype(BF16) for x, d in zip(approx, defect)]
    return approx


def lagrange(position):
    terms = []
    for k in range(4):
        value = None
        for m in range(4):
            if m != k:
                factor = (position - NODE_PLACES[m]) * (1.0 / (NODE_PLACES[k] - NODE_PLACES[m]))
                value = factor if value is None else value * factor
        terms.append(value)
    return terms


def pick(which, terms):
    return jnp.where(
        which == 0, terms[0], jnp.where(which == 1, terms[1], jnp.where(which == 2, terms[2], terms[3]))
    )


def main_kernel(
    jac_hbm,
    fc_hbm,
    om1_hbm,
    res_hbm,
    om_hbm,
    nb_hbm,
    don_hbm,
    rec_hbm,
    xyz_hbm,
    arrived,
    upd_hbm,
    owner_map,
    res_ref,
    om_ref,
    nb_ref,
    don_ref,
    rec_ref,
    xyz_ref,
    upd_ref,
    jac,
    inv,
    wire,
    fc,
    eye_ref,
    rhs_ref,
    acc_ref,
    guess_all,
    tails,
    faces,
    jac_sem,
    fc_sem,
    in_sem,
    upd_sem,
    own_sem,
    tails_sem,
    hs_sem,
    hr_sem,
    gs_sem,
    gr_sem,
    ts_sem,
    tr_sem,
):
    grid = lax.axis_index("grid")
    elem = lax.axis_index("elem")
    jac_copy = pltpu.make_async_copy(jac_hbm, jac, jac_sem)
    jac_copy.start()
    barrier = pltpu.get_barrier_semaphore()
    for i in range(GRIDS):
        if i != SELF:
            pl.semaphore_signal(
                barrier, inc=1, device_id={"grid": partner(i, grid)}, device_id_type=MESH
            )
    for k in range(1, ELEMS):
        pl.semaphore_signal(
            barrier, inc=1, device_id={"elem": (elem + k) % ELEMS}, device_id_type=MESH
        )

    small = ((om1_hbm, owner_map), (om_hbm, om_ref), (res_hbm, res_ref), (nb_hbm, nb_ref))
    small += ((don_hbm, don_ref), (rec_hbm, rec_ref), (xyz_hbm, xyz_ref))
    small_copies = [pltpu.make_async_copy(a, b, in_sem.at[k]) for k, (a, b) in enumerate(small)]
    for copy in small_copies:
        copy.start()
    fc_copy = pltpu.make_async_copy(fc_hbm, fc, fc_sem)
    fc_copy.start()

    def head_copy(i, h, place):
        rows = pl.ds(h * (HEAD // HALVES), HEAD // HALVES)
        return pltpu.make_async_remote_copy(
            src_ref=wire.at[i, rows],
            dst_ref=arrived.at[place, rows],
            send_sem=hs_sem.at[i, h],
            recv_sem=hr_sem.at[i, h],
            device_id={"grid": partner(i, grid)},
            device_id_type=MESH,
        )

    def tail_copy(i, place):
        return pltpu.make_async_remote_copy(
            src_ref=wire.at[i, pl.ds(HEAD, TAIL + PACK)],
            dst_ref=tails.at[place],
            send_sem=ts_sem.at[i],
            recv_sem=tr_sem.at[i],
            device_id={"grid": partner(i, grid)},
            device_id_type=MESH,
        )

    def guess_copy(k, place):
        return pltpu.make_async_remote_copy(
            src_ref=guess_all.at[elem],
            dst_ref=guess_all.at[place],
            send_sem=gs_sem.at[k],
            recv_sem=gr_sem.at[k],
            device_id={"elem": (elem + k) % ELEMS},
            device_id_type=MESH,
        )

    eye_ref[...] = jnp.where(iota((B, B), 0) == iota((B, B), 1), 1.0, 0.0)

    def partner_vector(i):
        j = i & 3
        dy = (1 + 2 * j - (j >> 1)) & 3
        dz = ((i >> 3) + 5 - dy) & 3
        dc = (i >> 2) & 1
        c, z, y = grid % 2, (grid // 2) % 4, grid // 8
        return (((y + dy) & 3) * 8 + ((z + dz) & 3) * 2 + ((c + dc) & 1)).astype(F32)

    for copy in small_copies:
        copy.wait()
    owner_row = om_ref[...].astype(F32)
    owner_col = column(om_ref[...])
    to_order = jnp.where(
        jnp.logical_and(owner_row == partner_vector(iota((128, SLOTS), 0)), iota((128, SLOTS), 0) < GRIDS), 1.0, 0.0
    )
    to_slot = jnp.where(
        jnp.logical_and(owner_col == partner_vector(iota((SLOTS, 128), 1)), iota((SLOTS, 128), 1) < GRIDS), 1.0, 0.0
    )
    live = jnp.sum(to_slot, axis=0, keepdims=True) > 0.0

    def ordered_columns(rows):
        ordered = dot(to_order.astype(BF16), rows).astype(BF16)
        return dot_t(eye_ref[...].astype(BF16), ordered).astype(BF16)

    rhs_ref[...] = ordered_columns(res_ref[...])
    acc_ref[...] = jnp.zeros((B, 128), F32)

    jac_copy.wait()

    def slot_of(i):
        wanted = partner(i, grid)
        slot = jnp.int32(0)
        for k in range(SLOTS):
            slot = jnp.where(owner_map[k] == wanted, jnp.int32(k), slot)
        return slot

    order_lane = iota((B, 128), 1)

    def build(first, count):
        places = [first + k for k in range(count)]
        results = invert([jac[slot_of(i)] for i in places], eye_ref[...])
        for i, result in zip(places, results):
            inv[i] = result
            wire[i, 0:320, :] = result[:, 0:128]
            wire[i, 320:640, :] = result[:, 128:256]
            wire[i, HEAD:WIRE, :] = jnp.concatenate([result[0:160, 256:320], result[160:320, 256:320]], axis=1)
        products = [dot(result, rhs_ref[...]) for result in results]
        total = acc_ref[...]
        for i, product in zip(places, products):
            total = jnp.where(order_lane == i, product, total)
        acc_ref[...] = total

    def build_group(q):
        for k in range(0, GROUP, TOGETHER):
            build(GROUP * q + k, TOGETHER)

    def send_half(q, h):
        for k in range(GROUP):
            if k != SELF % GROUP:
                head_copy(GROUP * q + k, h, grid).start()
                continue

            @pl.when(q != SELF // GROUP)
            def _():
                head_copy(GROUP * q + SELF % GROUP, h, grid).start()

    def send_group(q):
        for h in range(HALVES):
            send_half(q, h)

    build_group(0)
    pl.semaphore_wait(barrier, GRIDS - 1 + ELEMS - 1)
    send_group(0)

    def build_next(q, carry):
        build_group(q)

        @pl.when(q < 4)
        def _():
            send_group(q)

        @pl.when(q == 6)
        def _():
            send_group(4)

        return carry

    lax.fori_loop(1, GRIDS // GROUP, build_next, 0)

    guess = dot_t(to_slot.astype(BF16), jnp.where(live, acc_ref[...], 0.0).astype(BF16)).astype(BF16)
    guess_all[elem] = guess
    for k in range(1, ELEMS):
        guess_copy(k, elem).start()
    pack_row = iota((GRIDS * PACK, 2 * GRIDS), 0)
    pack_slot = pack_row & (PACK - 1)
    pack_kind = jnp.where(pack_slot >= 3, 1.0, 0.0)
    wanted_entry = 2.0 * partner_vector(pack_row >> 4) + pack_kind
    entry_lane = iota((GRIDS * PACK, 2 * GRIDS), 1).astype(F32)
    entries = jnp.where(wanted_entry == entry_lane, don_ref[...].astype(F32), 0.0)
    entry = jnp.sum(entries, axis=1, keepdims=True)
    used = (iota((GRIDS * PACK, SLOTS), 0) & (PACK - 1)) < 6
    donor_rows = jnp.where(used, one_hot(entry, SLOTS), 0.0).astype(BF16)
    wide = jnp.concatenate([guess, jnp.zeros((SLOTS, LANES - B), BF16)], axis=1)
    spread = dot(donor_rows, wide)
    row = iota((GRIDS * PACK, 128), 0) & (PACK - 1)
    third = jnp.where(row >= 3, row - 3, row)
    packed = jnp.where(
        third == 0, spread[:, 0:128], jnp.where(third == 1, spread[:, 128:256], spread[:, 256:384])
    )
    wire[:, WIRE : WIRE + PACK, :] = packed.astype(BF16).reshape(GRIDS, PACK, 128)
    tails[grid] = wire[SELF, HEAD : WIRE + PACK, :]

    def send_tails(i, carry):
        @pl.when(i != SELF)
        def _():
            tail_copy(i, grid).start()

        return carry

    lax.fori_loop(0, GRIDS, send_tails, 0)

    for h in range(HALVES):

        def send_rest(q, carry, h=h):
            send_half(q, h)
            return carry

        lax.fori_loop(EARLY, GRIDS // GROUP, send_rest, 0)
    own_copy = pltpu.make_async_copy(wire.at[SELF, pl.ds(0, HEAD)], arrived.at[grid, pl.ds(0, HEAD)], own_sem)
    own_copy.start()

    lane = iota((RPTS, B), 1)
    point = lane & (PTS - 1)
    xs = lagrange(column(xyz_ref[0:1, :]))
    ys = lagrange(column(xyz_ref[1:2, :]))
    zs = lagrange(column(xyz_ref[2:3, :]))
    basis = pick(point >> 4, xs) * pick((point >> 2) & 3, ys) * pick(point & 3, zs)
    at_point = point.astype(F32) == column(rec_ref[2:3, :])
    donor_col = column(rec_ref[0:1, :])
    donor_grid = jnp.floor(donor_col * 0.5)
    donor_base = PACK * donor_grid + 3.0 * (donor_col - 2.0 * donor_grid)
    target = jnp.where(
        rec_ref[1:2, :].astype(F32) == iota((SLOTS, RPTS), 0).astype(F32), 1.0, 0.0
    ).astype(BF16)
    same_var = jnp.where((iota((B, B), 0) >> 6) == (iota((B, B), 1) >> 6), 1.0, 0.0).astype(BF16)
    face_pick = jnp.concatenate(
        [one_hot(column(nb_ref[f : f + 1, :]), ELEMS * SLOTS) for f in range(6)], axis=0
    ).astype(BF16)

    fc_copy.wait()
    for k in range(1, ELEMS):
        guess_copy(k, (elem + ELEMS - k) % ELEMS).wait()
    rows = dot(face_pick, guess_all[...].reshape(ELEMS * SLOTS, B)).astype(BF16)
    faces[...] = dot(rows, fc[...])
    face_sum = jnp.zeros((SLOTS, B), F32)
    for f in range(6):
        opposite = f ^ 1
        part = faces[f * SLOTS : (f + 1) * SLOTS, opposite * B : (opposite + 1) * B]
        face_sum = face_sum + part.astype(BF16).astype(F32)

    def wait_tails(i, carry):
        @pl.when(i != SELF)
        def _():
            tail_copy(i, sender(i, grid)).wait()

        return carry

    lax.fori_loop(0, GRIDS, wait_tails, 0)
    tails_copy = pltpu.make_async_copy(
        tails.at[:, pl.ds(0, TAIL)], arrived.at[:, pl.ds(HEAD, TAIL)], tails_sem
    )
    tails_copy.start()
    packs = tails[:, TAIL : TAIL + PACK, :].reshape(GRIDS * PACK, 128)
    picked = jnp.concatenate(
        [dot(one_hot(donor_base + float(q), GRIDS * PACK).astype(BF16), packs) for q in range(3)], axis=1
    )[:, 0:B]
    values = two_term_left(picked * basis, same_var)
    fringe = two_term_dot(target, jnp.where(at_point, values, 0.0))
    sweep = (res_ref[...].astype(F32) - face_sum + fringe).astype(BF16)
    rhs_ref[...] = ordered_columns(sweep)

    def apply(q, carry):
        places = [GROUP * q + k for k in range(GROUP)]
        products = [dot(inv[i], rhs_ref[...]) for i in places]
        total = acc_ref[...]
        for i, product in zip(places, products):
            total = jnp.where(order_lane == i, product, total)
        acc_ref[...] = total
        return carry

    lax.fori_loop(0, GRIDS // GROUP, apply, 0)
    upd_ref[...] = lax.dot_general(
        to_slot,
        jnp.where(live, acc_ref[...], 0.0),
        (((1,), (1,)), ((), ())),
        precision=lax.Precision.HIGHEST,
        preferred_element_type=F32,
    )
    upd_copy = pltpu.make_async_copy(upd_ref, upd_hbm, upd_sem)
    upd_copy.start()
    own_copy.wait()
    upd_copy.wait()

    tails_copy.wait()

    def finish(i, carry):
        @pl.when(i != SELF)
        def _():
            for h in range(HALVES):
                head_copy(i, h, sender(i, grid)).wait()

        return carry

    lax.fori_loop(0, GRIDS, finish, 0)


def place_kernel(owned, upd_ref, w0, w1, w2, w3, out_ref, upd_out):
    for k, w in enumerate((w0, w1, w2, w3)):
        out_ref[k, :, 0:128] = w[0, 0:320, :]
        out_ref[k, :, 128:256] = w[0, 320:640, :]
        out_ref[k, 0:160, 256:320] = w[0, 640:800, 0:64]
        out_ref[k, 160:320, 256:320] = w[0, 640:800, 64:128]

    @pl.when(pl.program_id(0) == 0)
    def _():
        upd_out[...] = upd_ref[...]


def shards(jacobians, residual, owner_map, owner_slot, face_coupling, neighbours, donors, receptors, coords):
    anywhere = pl.BlockSpec(memory_space=pl.ANY)
    arrived, update = pl.pallas_call(
        main_kernel,
        out_shape=(
            jax.ShapeDtypeStruct((GRIDS, WIRE, 128), BF16),
            jax.ShapeDtypeStruct((SLOTS, B), F32),
        ),
        in_specs=[anywhere] * 9,
        out_specs=(anywhere, anywhere),
        scratch_shapes=[
            pltpu.SMEM((SLOTS,), jnp.int32),
            pltpu.VMEM((SLOTS, B), BF16),
            pltpu.VMEM((1, SLOTS), jnp.int32),
            pltpu.VMEM((6, SLOTS), jnp.int32),
            pltpu.VMEM((1, 2 * GRIDS), jnp.int32),
            pltpu.VMEM((3, RPTS), jnp.int32),
            pltpu.VMEM((3, RPTS), F32),
            pltpu.VMEM((SLOTS, B), F32),
            pltpu.VMEM((SLOTS, B, B), BF16),
            pltpu.VMEM((GRIDS, B, B), BF16),
            pltpu.VMEM((GRIDS, WIRE + PACK, 128), BF16),
            pltpu.VMEM((B, 6 * B), BF16),
            pltpu.VMEM((B, B), F32),
            pltpu.VMEM((B, 128), BF16),
            pltpu.VMEM((B, 128), F32),
            pltpu.VMEM((ELEMS, SLOTS, B), BF16),
            pltpu.VMEM((GRIDS, TAIL + PACK, 128), BF16),
            pltpu.VMEM((6 * SLOTS, 6 * B), F32),
            pltpu.SemaphoreType.DMA,
            pltpu.SemaphoreType.DMA,
            pltpu.SemaphoreType.DMA((7,)),
            pltpu.SemaphoreType.DMA,
            pltpu.SemaphoreType.DMA,
            pltpu.SemaphoreType.DMA,
            pltpu.SemaphoreType.DMA((GRIDS, HALVES)),
            pltpu.SemaphoreType.DMA((GRIDS, HALVES)),
            pltpu.SemaphoreType.DMA((ELEMS,)),
            pltpu.SemaphoreType.DMA((ELEMS,)),
            pltpu.SemaphoreType.DMA((GRIDS,)),
            pltpu.SemaphoreType.DMA((GRIDS,)),
        ],
        compiler_params=pltpu.CompilerParams(
            collective_id=0, has_side_effects=True, vmem_limit_bytes=60 * 2**20
        ),
        name="invert_send_sweep",
    )(
        jacobians,
        face_coupling,
        owner_map,
        residual,
        owner_map.reshape(1, SLOTS),
        neighbours,
        donors.reshape(1, 2 * GRIDS),
        receptors,
        coords,
    )

    def block(k):
        return pl.BlockSpec((1, WIRE, 128), lambda o, owned: (owned[4 * o + k], 0, 0))

    return pl.pallas_call(
        place_kernel,
        out_shape=(
            jax.ShapeDtypeStruct((OWN, B, B), BF16),
            jax.ShapeDtypeStruct((SLOTS, B), F32),
        ),
        grid_spec=pltpu.PrefetchScalarGridSpec(
            num_scalar_prefetch=1,
            grid=(OWN // 4,),
            in_specs=[pl.BlockSpec((SLOTS, B), lambda o, owned: (0, 0))] + [block(k) for k in range(4)],
            out_specs=(
                pl.BlockSpec((4, B, B), lambda o, owned: (o, 0, 0)),
                pl.BlockSpec((SLOTS, B), lambda o, owned: (0, 0)),
            ),
        ),
        name="place_owned",
    )(owner_slot, update, arrived, arrived, arrived, arrived)


def solution(mesh):
    in_specs = (
        P(("grid", "elem"), None, None),
        P(("grid", "elem"), None),
        P(("grid", "elem")),
        P(("grid", "elem")),
        P(),
        P(None, ("grid", "elem")),
        P(("grid", "elem")),
        P(None, ("grid", "elem")),
        P(None, ("grid", "elem")),
    )
    out_specs = (P(("grid", "elem"), None, None), P(("grid", "elem"), None))
    return jax.shard_map(shards, mesh=mesh, in_specs=in_specs, out_specs=out_specs, check_vma=False)
```
